32 devices in a mesh: dp: 4 (over y, x), mp: 8 (over z, core).
Axes of the slice: x: 2, y: 2, z: 4, core: 2. Of those that a mesh axis runs over, the one named last changes fastest.
Arguments:
- tokens: bfloat16 [512, 6144], P(('dp', 'mp')), may hold values from -6 to 6
- norm_gain: float32 [6144], replicated, may hold values from 0.5 to 1.5
- up_weight: bfloat16 [6144, 16384], P(None, 'mp'), may hold values from -0.078125 to 0.078125
- down_weight: bfloat16 [16384, 6144], P('mp'), may hold values from -0.046875 to 0.046875
- out_grad: bfloat16 [512, 6144], P(('dp', 'mp')), may hold values from -6 to 6
Outputs:
- input_grad: bfloat16 [512, 6144], P(('dp', 'mp'))
- up_grad: bfloat16 [6144, 16384], P('dp', 'mp')
- down_grad: bfloat16 [16384, 6144], P('mp', 'dp')
- gain_grad: float32 [6144], replicated
The draws below stay inside these ranges and needn't reach their ends.
All inputs are finite; a program needn't handle non-finite values.
Results may differ from the reference program's by a relative error of at most 0.018.
Values may be sent and summed in bfloat16 or wider, within the bound.
No kernel may reach another device: no remote copies, remote signals or barrier semaphores. Data moves between devices by JAX's collectives and lax.ppermute only.
A program may use at most 192 MiB of HBM per device.

```python
import math
import jax
import jax.numpy as jnp
from jax import lax

D = 6144
FF_WIN = 16384
TOK_GROUP = 128
TOKENS = 512
N_DP = 4


def block_levels(key, dims, split, least, high):
    def one(position, blocks):
        heights = jax.random.uniform(jax.random.fold_in(jax.random.fold_in(key, 6), position), (blocks,), jnp.float32, least / len(split), high / len(split))
        return jnp.repeat(jnp.exp(heights), dims[position] // blocks).reshape((-1,) + (1,) * (len(dims) - position - 1))

    loudness = one(*split[0])
    for cut in split[1:]:
        loudness = loudness * one(*cut)
    return loudness


def bell_draw(key, shape, deviation, bound, cuts=(), kind=jnp.bfloat16):
    result = deviation * jax.random.normal(key, shape, jnp.float32)
    if cuts:
        result = result * block_levels(key, shape, cuts, -0.22, 0.18)
    return jnp.clip(result, -bound, bound).astype(kind)


def setup_inputs(seed: int = 0) -> dict:
    arg_keys = jax.random.split(jax.random.key(seed), 6)
    tokens = bell_draw(arg_keys[0], (TOKENS, D), 1.0, 6.0, ((0, 32),))
    norm_gain = jnp.clip(1.0 + 0.1 * jax.random.normal(arg_keys[1], (D,), jnp.float32), 0.5, 1.5)
    up_weight = bell_draw(arg_keys[2], (D, FF_WIN), D ** -0.5, 0.078125, ((1, 8),))
    down_weight = bell_draw(arg_keys[3], (FF_WIN, D), FF_WIN ** -0.5, 0.046875, ((0, 8),))
    out_grad = bell_draw(arg_keys[4], (TOKENS, D), 1.0, 6.0, ((0, 32),))
    return dict(tokens=tokens, norm_gain=norm_gain, up_weight=up_weight, down_weight=down_weight, out_grad=out_grad)


def gelu_value(preact):
    return 0.5 * preact * (1.0 + lax.erf(preact * 0.7071067811865476))

def gelu_slope(preact):
    return 0.5 * (1.0 + lax.erf(preact * 0.7071067811865476)) + preact * jnp.exp(-0.5 * preact * preact) * 0.3989422804014327

def reference(tokens, norm_gain, up_weight, down_weight, out_grad):
    values = tokens.astype(jnp.float32)
    centered = values - lax.optimization_barrier(jnp.mean(values, axis=1, keepdims=True))
    inv_std = lax.rsqrt(lax.optimization_barrier(jnp.mean(centered * centered, axis=1, keepdims=True)) + 1e-06)
    x_hat = centered * inv_std
    normed = (x_hat * norm_gain).astype(jnp.bfloat16)
    preact = jnp.dot(normed, up_weight, preferred_element_type=jnp.float32)
    hidden = gelu_value(preact).astype(jnp.bfloat16)
    hid_grad = jnp.dot(out_grad, down_weight.T, preferred_element_type=jnp.float32)
    pre_grad = (hid_grad * gelu_slope(preact)).astype(jnp.bfloat16)
    norm_grad = jnp.dot(pre_grad, up_weight.T, preferred_element_type=jnp.float32)
    factor = 1.0 / math.sqrt(TOKENS)
    gain_grad = lax.optimization_barrier(jnp.sum(norm_grad * x_hat, axis=0)) * factor
    scaled = norm_gain * norm_grad
    input_grad = (scaled - lax.optimization_barrier(jnp.mean(scaled, axis=1, keepdims=True)) - x_hat * lax.optimization_barrier(jnp.mean(scaled * x_hat, axis=1, keepdims=True))) * inv_std
    up_total = jnp.zeros((D, FF_WIN), jnp.float32)
    down_total = jnp.zeros((FF_WIN, D), jnp.float32)
    for replica in range(N_DP):
        first = replica * TOK_GROUP
        last = first + TOK_GROUP
        up_part = jnp.dot(normed[first:last].T, pre_grad[first:last], preferred_element_type=jnp.float32)
        down_part = jnp.dot(hidden[first:last].T, out_grad[first:last], preferred_element_type=jnp.float32)
        up_total = up_total + up_part.astype(jnp.bfloat16).astype(jnp.float32)
        down_total = down_total + down_part.astype(jnp.bfloat16).astype(jnp.float32)
    up_grad = (up_total * factor).astype(jnp.bfloat16)
    down_grad = (down_total * factor).astype(jnp.bfloat16)
    return (input_grad.astype(jnp.bfloat16), up_grad, down_grad, gain_grad)
```

```python
import math

import jax
import jax.numpy as jnp
from jax import lax
from jax.sharding import PartitionSpec as P


def gelu_value(preact):
    return 0.5 * preact * (1.0 + lax.erf(preact * 0.7071067811865476))


def gelu_slope(preact):
    return (
        0.5 * (1.0 + lax.erf(preact * 0.7071067811865476))
        + preact * jnp.exp(-0.5 * preact * preact) * 0.3989422804014327
    )


def swap_perm(size, mask):
    return [(i, i ^ mask) for i in range(size)]


def ring_perm(size, shift):
    chips = size // 2
    order = list(range(0, chips, 2)) + list(range(1, chips, 2))[::-1]
    moved = {order[k]: order[(k + shift) % chips] for k in range(chips)}
    return [(2 * c + core, 2 * moved[c] + core) for c in range(chips) for core in range(2)]


def contract(a, b, dims):
    return lax.dot_general(a, b, (dims, ((), ())), preferred_element_type=jnp.float32)


def per_device(tokens, norm_gain, up_weight, down_weight, out_grad):
    n_dp, n_mp = lax.axis_size("dp"), lax.axis_size("mp")
    chips = n_mp // 2
    rows, width = tokens.shape
    cols = width // n_dp
    me = lax.axis_index("dp")
    factor = 1.0 / math.sqrt(rows * n_mp * n_dp)

    def along_ring(array, shift=1):
        return lax.ppermute(array, "mp", ring_perm(n_mp, shift))

    def across(array):
        return lax.ppermute(array, "mp", swap_perm(n_mp, 1))

    def replica(array, mask):
        return lax.ppermute(array, "dp", swap_perm(n_dp, mask))

    def spread(own):
        pieces = [own]
        for _ in range(chips - 1):
            pieces.append(along_ring(pieces[-1]))
        return pieces, [across(p) for p in pieces]

    def replicas(own, low):
        out = [own]
        for k in range(1, n_dp):
            bit = (k & -k) if low else 1 << (k.bit_length() - 1)
            out.append(replica(out[k ^ bit], bit))
        return out

    values = tokens.astype(jnp.float32)
    centered = values - jnp.mean(values, axis=1, keepdims=True)
    inv_std = lax.rsqrt(jnp.mean(centered * centered, axis=1, keepdims=True) + 1e-06)
    x_hat = centered * inv_std
    normed = (x_hat * norm_gain).astype(jnp.bfloat16)

    cotan_mine, cotan_other = spread(out_grad)
    normed_mine, normed_other = spread(normed)
    normed_all = jnp.concatenate(normed_mine + normed_other, axis=0)
    cotan_all = jnp.concatenate(cotan_mine + cotan_other, axis=0)

    def block_of(array, k):
        return lax.dynamic_slice_in_dim(array, (me ^ k) * cols, cols, axis=1)

    def column_shards(k):
        both = jnp.stack([block_of(normed, k), block_of(out_grad, k)])
        return replica(both, k) if k else both

    shard = jnp.stack([column_shards(k) for k in range(n_dp)])
    shards_mine, shards_other = spread(shard)
    columns = jnp.stack([jnp.stack(shards_mine), jnp.stack(shards_other)])
    columns = columns.transpose(3, 2, 0, 1, 4, 5).reshape(2, -1, cols)

    preact = contract(normed_all, up_weight, ((1,), (0,)))
    hidden = gelu_value(preact).astype(jnp.bfloat16)
    hid_grad = contract(cotan_all, down_weight, ((1,), (1,)))
    pre_grad = (hid_grad * gelu_slope(preact)).astype(jnp.bfloat16)
    partial = contract(pre_grad, up_weight, ((1,), (1,))).astype(jnp.bfloat16)

    hidden_all = jnp.concatenate(replicas(hidden, True), axis=0)
    pre_all = jnp.concatenate(replicas(pre_grad, False), axis=0)

    x_hat_all = normed_all.astype(jnp.float32) / norm_gain
    gain_grad = jnp.sum(partial.astype(jnp.float32) * x_hat_all, axis=0)
    for bit in range((n_dp - 1).bit_length()):
        gain_grad = gain_grad + replica(gain_grad, 1 << bit)
    gain_grad = gain_grad + across(gain_grad)
    shift = 1
    while shift < chips:
        gain_grad = gain_grad + along_ring(gain_grad, shift)
        shift *= 2
    gain_grad = gain_grad * factor

    half = rows * chips
    total = partial[:half].astype(jnp.float32) + across(partial[half:]).astype(jnp.float32)
    parts = total.astype(jnp.bfloat16).reshape(chips, rows, width)
    norm_grad = total[:rows]
    for s in range(1, chips):
        norm_grad = norm_grad + along_ring(parts[s], -s).astype(jnp.float32)
    scaled = norm_gain * norm_grad
    input_grad = (
        scaled
        - jnp.mean(scaled, axis=1, keepdims=True)
        - x_hat * jnp.mean(scaled * x_hat, axis=1, keepdims=True)
    ) * inv_std

    down_grad = (contract(hidden_all, columns[1], ((0,), (0,))) * factor).astype(jnp.bfloat16)
    up_grad = (contract(columns[0], pre_all, ((0,), (0,))) * factor).astype(jnp.bfloat16)
    return (input_grad.astype(jnp.bfloat16), up_grad, down_grad, gain_grad)


def solution(mesh):
    placed = (P(("dp", "mp"), None), P(), P(None, "mp"), P("mp", None), P(("dp", "mp"), None))
    return jax.shard_map(
        per_device,
        mesh=mesh,
        in_specs=placed,
        out_specs=(P(("dp", "mp"), None), P("dp", "mp"), P("mp", "dp"), P()),
        check_vma=False,
    )
```

```python
import math

import jax
import jax.numpy as jnp
from jax import lax
from jax.sharding import PartitionSpec as P


def gelu_value(preact):
    return 0.5 * preact * (1.0 + lax.erf(preact * 0.7071067811865476))


def gelu_slope(preact):
    return (
        0.5 * (1.0 + lax.erf(preact * 0.7071067811865476))
        + preact * jnp.exp(-0.5 * preact * preact) * 0.3989422804014327
    )


def swap_perm(size, mask):
    return [(i, i ^ mask) for i in range(size)]


def ring_perm(size, shift):
    chips = size // 2
    order = list(range(0, chips, 2)) + list(range(1, chips, 2))[::-1]
    moved = {order[k]: order[(k + shift) % chips] for k in range(chips)}
    return [(2 * c + core, 2 * moved[c] + core) for c in range(chips) for core in range(2)]


def contract(a, b, dims):
    return lax.dot_general(a, b, (dims, ((), ())), preferred_element_type=jnp.float32)


def layer(tokens, norm_gain, up_weight, down_weight, out_grad):
    n_dp, n_mp = lax.axis_size("dp"), lax.axis_size("mp")
    chips = n_mp // 2
    rows, width = tokens.shape
    cols = width // n_dp
    me = lax.axis_index("dp")
    factor = 1.0 / math.sqrt(rows * n_mp * n_dp)

    def along_ring(array, shift=1):
        return lax.ppermute(array, "mp", ring_perm(n_mp, shift))

    def across(array):
        return lax.ppermute(array, "mp", swap_perm(n_mp, 1))

    def replica(array, mask):
        return lax.ppermute(array, "dp", swap_perm(n_dp, mask))

    def spread(own):
        pieces = [own]
        for _ in range(1, chips):
            pieces.append(along_ring(pieces[-1]))
        return pieces, [across(p) for p in pieces]

    def replicas(own, low):
        out = [own]
        for k in range(1, n_dp):
            bit = (k & -k) if low else 1 << (k.bit_length() - 1)
            out.append(replica(out[k ^ bit], bit))
        return out

    values = tokens.astype(jnp.float32)
    centered = values - jnp.mean(values, axis=1, keepdims=True)
    inv_std = lax.rsqrt(jnp.mean(centered * centered, axis=1, keepdims=True) + 1e-06)
    x_hat = centered * inv_std
    normed = (x_hat * norm_gain).astype(jnp.bfloat16)

    cotan_mine, cotan_other = spread(out_grad)
    normed_mine, normed_other = spread(normed)
    normed_all = jnp.concatenate(normed_mine + normed_other, axis=0)
    cotan_all = jnp.concatenate(cotan_mine + cotan_other, axis=0)

    def block_of(array, k):
        return lax.dynamic_slice_in_dim(array, (me ^ k) * cols, cols, axis=1)

    def column_shards(k):
        both = jnp.stack([block_of(normed, k), block_of(out_grad, k)])
        return replica(both, k) if k else both

    shard_list = [column_shards(k) for k in range(n_dp)]
    shard = jnp.stack(shard_list)
    shards_mine, shards_other = spread(shard)
    columns = jnp.stack([jnp.stack(shards_mine), jnp.stack(shards_other)])
    columns = columns.transpose(3, 2, 0, 1, 4, 5).reshape(2, -1, cols)

    preact = contract(normed_all, up_weight, ((1,), (0,)))
    hidden = gelu_value(preact).astype(jnp.bfloat16)
    hid_grad = contract(cotan_all, down_weight, ((1,), (1,)))
    pre_grad = (hid_grad * gelu_slope(preact)).astype(jnp.bfloat16)
    partial = contract(pre_grad, up_weight, ((1,), (1,))).astype(jnp.bfloat16)
    x_hat_all = normed_all.astype(jnp.float32) / norm_gain
    gain_grad = jnp.sum(partial.astype(jnp.float32) * x_hat_all, axis=0)

    hidden_all = jnp.concatenate(replicas(hidden, True), axis=0)
    pre_all = jnp.concatenate(replicas(pre_grad, False), axis=0)

    for bit in range((n_dp - 1).bit_length()):
        gain_grad = gain_grad + replica(gain_grad, 1 << bit)
    gain_grad = gain_grad + across(gain_grad)
    shift = 1
    while shift < chips:
        gain_grad = gain_grad + along_ring(gain_grad, shift)
        shift *= 2
    gain_grad = gain_grad * factor

    half = rows * chips
    total = partial[:half].astype(jnp.float32) + across(partial[half:]).astype(jnp.float32)
    parts = total.astype(jnp.bfloat16).reshape(chips, rows, width)
    norm_grad = total[:rows]
    for s in range(1, chips):
        norm_grad = norm_grad + along_ring(parts[s], -s).astype(jnp.float32)
    scaled = norm_gain * norm_grad
    input_grad = (
        scaled
        - jnp.mean(scaled, axis=1, keepdims=True)
        - x_hat * jnp.mean(scaled * x_hat, axis=1, keepdims=True)
    ) * inv_std

    down_grad = (contract(hidden_all, columns[1], ((0,), (0,))) * factor).astype(jnp.bfloat16)
    up_grad = (contract(columns[0], pre_all, ((0,), (0,))) * factor).astype(jnp.bfloat16)
    return (input_grad.astype(jnp.bfloat16), up_grad, down_grad, gain_grad)


def solution(mesh):
    placed = (P(("dp", "mp"), None), P(), P(None, "mp"), P("mp", None), P(("dp", "mp"), None))
    return jax.shard_map(
        layer,
        mesh=mesh,
        in_specs=placed,
        out_specs=(P(("dp", "mp"), None), P("dp", "mp"), P("mp", "dp"), P()),
        check_vma=False,
    )
```

```python
import functools
import math

import jax
import jax.numpy as jnp
from jax import lax
from jax.experimental import pallas as pl
from jax.experimental.pallas import tpu as pltpu
from jax.sharding import PartitionSpec as P


def gelu_value(preact):
    return 0.5 * preact * (1.0 + lax.erf(preact * 0.7071067811865476))


def gelu_slope(preact):
    return (
        0.5 * (1.0 + lax.erf(preact * 0.7071067811865476))
        + preact * jnp.exp(-0.5 * preact * preact) * 0.3989422804014327
    )


def swap_perm(size, mask):
    return [(i, i ^ mask) for i in range(size)]


def ring_perm(size, shift):
    chips = size // 2
    order = list(range(0, chips, 2)) + list(range(1, chips, 2))[::-1]
    moved = {order[k]: order[(k + shift) % chips] for k in range(chips)}
    return [(2 * c + core, 2 * moved[c] + core) for c in range(chips) for core in range(2)]


def contract(a, b, dims):
    return lax.dot_general(a, b, (dims, ((), ())), preferred_element_type=jnp.float32)


def normalise(values, gain):
    values = values.astype(jnp.float32)
    centered = values - jnp.mean(values, axis=1, keepdims=True)
    inv_std = lax.rsqrt(jnp.mean(centered * centered, axis=1, keepdims=True) + 1e-06)
    x_hat = centered * inv_std
    return (x_hat * gain).astype(jnp.bfloat16), x_hat, inv_std


def chunk(total, most, unit):
    for parts in range(1, total // unit + 1):
        if total % parts == 0 and total // parts <= most and (total // parts) % unit == 0:
            return total // parts
    return total


WHOLE = pl.BlockSpec(memory_space=pltpu.VMEM)
STAYS = pl.BlockSpec(memory_space=pl.ANY)


class Stream:
    def __init__(self, weight, buffer, sems, step):
        self.refs, self.sems, self.step = (weight, buffer), sems, step

    def copy(self, part):
        start = part * self.step
        if not isinstance(part, int):
            start = pl.multiple_of(start, self.step)
        rows = pl.ds(start, self.step)
        return pltpu.make_async_copy(self.refs[0].at[rows], self.refs[1].at[rows], self.sems.at[part])

    def start(self):
        for part in range(self.refs[0].shape[0] // self.step):
            self.copy(part).start()


def call(kernel, operands, in_specs, outs, weight, step, extra=()):
    rows, width = weight.shape
    return pl.pallas_call(
        kernel,
        in_specs=in_specs,
        out_specs=[WHOLE] * len(outs),
        out_shape=[jax.ShapeDtypeStruct(*o) for o in outs],
        scratch_shapes=[
            pltpu.VMEM((rows, width), weight.dtype),
            pltpu.SemaphoreType.DMA((rows // step,)),
            *extra,
        ],
        compiler_params=pltpu.CompilerParams(vmem_limit_bytes=60 * 2**20),
        cost_estimate=pl.CostEstimate(
            flops=2 * rows * width * outs[0][0][0], bytes_accessed=2 * rows * width, transcendentals=0
        ),
    )(*operands)


def norm_kernel(parts, tokens, cotan, gain, x_hat, scale, blocks):
    normed, x_hat[...], inv_std = normalise(tokens[...], gain[...])
    scale[...] = jnp.broadcast_to(inv_std, scale.shape)
    cols = normed.shape[1] // parts
    for part in range(parts):
        span = slice(part * cols, (part + 1) * cols)
        blocks[part, 0] = normed[:, span]
        blocks[part, 1] = cotan[:, span]


def preact_kernel(step, count, *refs):
    pieces, (gain, weight, hidden, slope, normed, buffer, sems, total) = refs[:count], refs[count:]
    stream = Stream(weight, buffer, sems, step)
    stream.start()
    row = 0
    for piece in pieces:
        normed[row : row + piece.shape[0], :] = normalise(piece[...], gain[...])[0]
        row += piece.shape[0]
    total[...] = jnp.zeros_like(total)

    def body(part, carry):
        stream.copy(part).wait()
        span = pl.ds(pl.multiple_of(part * step, step), step)
        total[...] += contract(normed[:, span], buffer[span, :], ((1,), (0,)))
        return carry

    lax.fori_loop(0, weight.shape[0] // step, body, 0)
    hidden[...] = gelu_value(total[...]).astype(jnp.bfloat16)
    slope[...] = gelu_slope(total[...])


def hidgrad_kernel(step, span_of, count, *refs):
    pieces, (weight, slope, pre, buffer, sems, cotan) = refs[:count], refs[count:]
    stream = Stream(weight, buffer, sems, step)
    stream.start()
    row = 0
    for piece in pieces:
        cotan[row : row + piece.shape[0], :] = piece[...]
        row += piece.shape[0]

    def body(part, carry):
        for inner in range(span_of // step):
            stream.copy(part * (span_of // step) + inner).wait()
        span = pl.ds(pl.multiple_of(part * span_of, span_of), span_of)
        hid_grad = contract(buffer[span, :], cotan[...], ((1,), (1,))).T
        pre[:, span] = (hid_grad * slope[:, span]).astype(jnp.bfloat16)
        return carry

    lax.fori_loop(0, weight.shape[0] // span_of, body, 0)


def normgrad_kernel(step, pre, weight, normed, gain, partial, gain_part, buffer, sems):
    stream = Stream(weight, buffer, sems, step)
    stream.start()

    def body(part, carry):
        stream.copy(part).wait()
        span = pl.ds(pl.multiple_of(part * step, step), step)
        grad = contract(pre[...], buffer[span, :], ((1,), (1,)))
        partial[:, span] = grad.astype(jnp.bfloat16)
        x_hat = normed[:, span].astype(jnp.float32) / gain[:, span]
        gain_part[:, span] = jnp.sum(grad * x_hat, axis=0, keepdims=True)
        return carry

    lax.fori_loop(0, weight.shape[0] // step, body, 0)


def layer(tokens, norm_gain, up_weight, down_weight, out_grad):
    n_dp, n_mp = lax.axis_size("dp"), lax.axis_size("mp")
    chips = n_mp // 2
    rows, width = tokens.shape
    units = up_weight.shape[1]
    group = rows * n_mp
    cols = width // n_dp
    me = lax.axis_index("dp")
    factor = 1.0 / math.sqrt(group * n_dp)

    def along_ring(array, shift=1):
        return lax.ppermute(array, "mp", ring_perm(n_mp, shift))

    def across(array):
        return lax.ppermute(array, "mp", swap_perm(n_mp, 1))

    def replica(array, mask):
        return lax.ppermute(array, "dp", swap_perm(n_dp, mask))

    def spread(own):
        pieces = [own]
        for _ in range(1, chips):
            pieces.append(along_ring(pieces[-1]))
        return pieces, [across(p) for p in pieces]

    def gathered(own):
        mine, other = spread(own)
        return mine + other if rows % 16 == 0 else [jnp.concatenate(mine + other, axis=0)]

    def replicas(own, low):
        out = [own]
        for k in range(1, n_dp):
            bit = (k & -k) if low else 1 << (k.bit_length() - 1)
            out.append(replica(out[k ^ bit], bit))
        return out

    token_pieces = gathered(tokens)
    cotan_pieces = gathered(out_grad)
    gain_row = norm_gain.reshape(1, width)
    x_hat, scale, blocks = pl.pallas_call(
        functools.partial(norm_kernel, n_dp),
        in_specs=[WHOLE] * 3,
        out_specs=[WHOLE] * 3,
        out_shape=[
            jax.ShapeDtypeStruct((rows, width), jnp.float32),
            jax.ShapeDtypeStruct((rows, 128), jnp.float32),
            jax.ShapeDtypeStruct((n_dp, 2, rows, cols), jnp.bfloat16),
        ],
        name="ln",
    )(tokens, out_grad, gain_row)
    inv_std = scale[:, :1]

    def column_shards(k):
        both = lax.dynamic_index_in_dim(blocks, me ^ k, 0, keepdims=False)
        return replica(both, k) if k else both

    shard_list = [column_shards(k) for k in range(n_dp)]
    shard = jnp.stack(shard_list)
    shards_mine, shards_other = spread(shard)
    columns = jnp.stack([jnp.stack(shards_mine), jnp.stack(shards_other)])
    columns = columns.transpose(3, 2, 0, 1, 4, 5).reshape(2, -1, cols)
    normed_cols, cotan_cols = columns[0], columns[1]

    float_units, half_units = ((group, units), jnp.float32), ((group, units), jnp.bfloat16)
    half_width = ((group, width), jnp.bfloat16)
    step, count = chunk(width, 384, 128), len(token_pieces)
    hidden, slope, normed_all = call(
        functools.partial(preact_kernel, step, count),
        (*token_pieces, gain_row, up_weight),
        [WHOLE] * (count + 1) + [STAYS],
        (half_units, float_units, half_width),
        up_weight,
        step,
        (pltpu.VMEM(*float_units),),
    )
    span_of, count = chunk(units, 512, 128), len(cotan_pieces)
    step = chunk(span_of, 256, 128)
    (pre_grad,) = call(
        functools.partial(hidgrad_kernel, step, span_of, count),
        (*cotan_pieces, down_weight, slope),
        [WHOLE] * count + [STAYS, WHOLE],
        (half_units,),
        down_weight,
        step,
        (pltpu.VMEM(*half_width),),
    )
    step = chunk(width, 768, 128)
    partial, gain_grad = call(
        functools.partial(normgrad_kernel, step),
        (pre_grad, up_weight, normed_all, gain_row),
        [WHOLE, STAYS, WHOLE, WHOLE],
        (half_width, ((1, width), jnp.float32)),
        up_weight,
        step,
    )

    hidden_all = jnp.concatenate(replicas(hidden, True), axis=0)
    pre_all = jnp.concatenate(replicas(pre_grad, False), axis=0)

    gain_grad = gain_grad + across(gain_grad)
    shift = 1
    while shift < chips:
        gain_grad = gain_grad + along_ring(gain_grad, shift)
        shift *= 2
    for bit in range((n_dp - 1).bit_length()):
        gain_grad = gain_grad + replica(gain_grad, 1 << bit)
    gain_grad = gain_grad.reshape(width) * factor

    half = rows * chips
    total = partial[:half].astype(jnp.float32) + across(partial[half:]).astype(jnp.float32)
    parts = total.astype(jnp.bfloat16).reshape(chips, rows, width)
    norm_grad = total[:rows]
    for s in range(1, chips):
        norm_grad = norm_grad + along_ring(parts[s], -s).astype(jnp.float32)
    scaled = norm_gain * norm_grad
    input_grad = (
        scaled
        - jnp.mean(scaled, axis=1, keepdims=True)
        - x_hat * jnp.mean(scaled * x_hat, axis=1, keepdims=True)
    ) * inv_std

    down_grad = (contract(hidden_all, cotan_cols, ((0,), (0,))) * factor).astype(jnp.bfloat16)
    up_grad = (contract(normed_cols, pre_all, ((0,), (0,))) * factor).astype(jnp.bfloat16)
    return (input_grad.astype(jnp.bfloat16), up_grad, down_grad, gain_grad)


def solution(mesh):
    placed = (P(("dp", "mp"), None), P(), P(None, "mp"), P("mp", None), P(("dp", "mp"), None))
    return jax.shard_map(
        layer,
        mesh=mesh,
        in_specs=placed,
        out_specs=(P(("dp", "mp"), None), P("dp", "mp"), P("mp", "dp"), P()),
        check_vma=False,
    )
```

```python
import functools
import math

import jax
import jax.numpy as jnp
from jax import lax
from jax.experimental import pallas as pl
from jax.experimental.pallas import tpu as pltpu
from jax.sharding import PartitionSpec as P


def gelu_value(preact):
    return 0.5 * preact * (1.0 + lax.erf(preact * 0.7071067811865476))


def gelu_slope(preact):
    return (
        0.5 * (1.0 + lax.erf(preact * 0.7071067811865476))
        + preact * jnp.exp(-0.5 * preact * preact) * 0.3989422804014327
    )


def swap_perm(size, mask):
    return [(i, i ^ mask) for i in range(size)]


def ring_perm(size, shift):
    chips = size // 2
    order = list(range(0, chips, 2)) + list(range(1, chips, 2))[::-1]
    moved = {order[k]: order[(k + shift) % chips] for k in range(chips)}
    return [(2 * c + core, 2 * moved[c] + core) for c in range(chips) for core in range(2)]


def contract(a, b, dims):
    return lax.dot_general(a, b, (dims, ((), ())), preferred_element_type=jnp.float32)


def normalise(values, gain):
    values = values.astype(jnp.float32)
    centered = values - jnp.mean(values, axis=1, keepdims=True)
    inv_std = lax.rsqrt(jnp.mean(centered * centered, axis=1, keepdims=True) + 1e-06)
    x_hat = centered * inv_std
    return (x_hat * gain).astype(jnp.bfloat16), x_hat, inv_std


def chunk(total, most, unit):
    for parts in range(1, total // unit + 1):
        if total % parts == 0 and total // parts <= most and (total // parts) % unit == 0:
            return total // parts
    return total


WHOLE = pl.BlockSpec(memory_space=pltpu.VMEM)
STAYS = pl.BlockSpec(memory_space=pl.ANY)


class Stream:
    def __init__(self, weight, buffer, sems, step):
        self.refs, self.sems, self.step = (weight, buffer), sems, step

    def copy(self, part):
        start = part * self.step
        if not isinstance(part, int):
            start = pl.multiple_of(start, self.step)
        rows = pl.ds(start, self.step)
        return pltpu.make_async_copy(self.refs[0].at[rows], self.refs[1].at[rows], self.sems.at[part])

    def start(self):
        for part in range(self.refs[0].shape[0] // self.step):
            self.copy(part).start()


def call(kernel, operands, in_specs, outs, weight, step, extra=()):
    rows, width = weight.shape
    return pl.pallas_call(
        kernel,
        in_specs=in_specs,
        out_specs=[WHOLE] * len(outs),
        out_shape=[jax.ShapeDtypeStruct(*o) for o in outs],
        scratch_shapes=[
            pltpu.VMEM((rows, width), weight.dtype),
            pltpu.SemaphoreType.DMA((rows // step,)),
            *extra,
        ],
        compiler_params=pltpu.CompilerParams(vmem_limit_bytes=60 * 2**20),
        cost_estimate=pl.CostEstimate(
            flops=2 * rows * width * outs[0][0][0], bytes_accessed=2 * rows * width, transcendentals=0
        ),
    )(*operands)


def norm_kernel(parts, tokens, cotan, gain, x_hat, scale, blocks):
    normed, x_hat[...], inv_std = normalise(tokens[...], gain[...])
    scale[...] = jnp.broadcast_to(inv_std, scale.shape)
    cols = normed.shape[1] // parts
    for part in range(parts):
        span = slice(part * cols, (part + 1) * cols)
        blocks[part, 0] = normed[:, span]
        blocks[part, 1] = cotan[:, span]


def preact_kernel(step, count, *refs):
    pieces, (gain, weight, hidden, slope, normed, buffer, sems, total) = refs[:count], refs[count:]
    stream = Stream(weight, buffer, sems, step)
    stream.start()
    row = 0
    for piece in pieces:
        normed[row : row + piece.shape[0], :] = normalise(piece[...], gain[...])[0]
        row += piece.shape[0]
    total[...] = jnp.zeros_like(total)

    def body(part, carry):
        stream.copy(part).wait()
        span = pl.ds(pl.multiple_of(part * step, step), step)
        total[...] += contract(normed[:, span], buffer[span, :], ((1,), (0,)))
        return carry

    lax.fori_loop(0, weight.shape[0] // step, body, 0)
    hidden[...] = gelu_value(total[...]).astype(jnp.bfloat16)
    slope[...] = gelu_slope(total[...])


def hidgrad_kernel(step, span_of, count, *refs):
    pieces, (weight, slope, pre, buffer, sems, cotan) = refs[:count], refs[count:]
    stream = Stream(weight, buffer, sems, step)
    stream.start()
    row = 0
    for piece in pieces:
        cotan[row : row + piece.shape[0], :] = piece[...]
        row += piece.shape[0]

    def body(part, carry):
        for inner in range(span_of // step):
            stream.copy(part * (span_of // step) + inner).wait()
        span = pl.ds(pl.multiple_of(part * span_of, span_of), span_of)
        hid_grad = contract(buffer[span, :], cotan[...], ((1,), (1,))).T
        pre[:, span] = (hid_grad * slope[:, span]).astype(jnp.bfloat16)
        return carry

    lax.fori_loop(0, weight.shape[0] // span_of, body, 0)


def normgrad_kernel(step, pre, weight, normed, gain, mine, other, gain_part, buffer, sems):
    half = mine.shape[0]
    stream = Stream(weight, buffer, sems, step)
    stream.start()

    def body(part, carry):
        stream.copy(part).wait()
        span = pl.ds(pl.multiple_of(part * step, step), step)
        grad = contract(pre[...], buffer[span, :], ((1,), (1,)))
        mine[:, span] = grad[:half].astype(jnp.bfloat16)
        other[:, span] = grad[half:].astype(jnp.bfloat16)
        x_hat = normed[:, span].astype(jnp.float32) / gain[:, span]
        gain_part[:, span] = jnp.sum(grad * x_hat, axis=0, keepdims=True)
        return carry

    lax.fori_loop(0, weight.shape[0] // step, body, 0)


def layer(tokens, norm_gain, up_weight, down_weight, out_grad):
    n_dp, n_mp = lax.axis_size("dp"), lax.axis_size("mp")
    chips = n_mp // 2
    rows, width = tokens.shape
    units = up_weight.shape[1]
    group = rows * n_mp
    cols = width // n_dp
    me = lax.axis_index("dp")
    factor = 1.0 / math.sqrt(group * n_dp)

    def along_ring(array, shift=1):
        return lax.ppermute(array, "mp", ring_perm(n_mp, shift))

    def across(array):
        return lax.ppermute(array, "mp", swap_perm(n_mp, 1))

    def replica(array, mask):
        return lax.ppermute(array, "dp", swap_perm(n_dp, mask))

    def spread(own, relayed):
        pieces = [own]
        for s in range(1, chips):
            if relayed:
                pieces.append(along_ring(pieces[-1]))
            else:
                pieces.append(along_ring(own, s))
        return pieces, [across(p) for p in pieces]

    def gathered(own, relayed):
        mine, other = spread(own, relayed)
        return mine + other if rows % 16 == 0 else [jnp.concatenate(mine + other, axis=0)]

    def replicas(own, low):
        out = [own]
        for k in range(1, n_dp):
            bit = (k & -k) if low else 1 << (k.bit_length() - 1)
            out.append(replica(out[k ^ bit], bit))
        return out

    token_pieces = gathered(tokens, True)
    cotan_pieces = gathered(out_grad, False)
    gain_row = norm_gain.reshape(1, width)
    x_hat, scale, blocks = pl.pallas_call(
        functools.partial(norm_kernel, n_dp),
        in_specs=[WHOLE] * 3,
        out_specs=[WHOLE] * 3,
        out_shape=[
            jax.ShapeDtypeStruct((rows, width), jnp.float32),
            jax.ShapeDtypeStruct((rows, 128), jnp.float32),
            jax.ShapeDtypeStruct((n_dp, 2, rows, cols), jnp.bfloat16),
        ],
        name="ln",
    )(tokens, out_grad, gain_row)
    inv_std = scale[:, :1]

    def column_shards(k):
        both = lax.dynamic_index_in_dim(blocks, me ^ k, 0, keepdims=False)
        return replica(both, k) if k else both

    shard_list = [column_shards(k) for k in range(n_dp)]
    shard = jnp.stack(shard_list)
    shards_mine, shards_other = spread(shard, False)
    columns = jnp.stack([jnp.stack(shards_mine), jnp.stack(shards_other)])
    columns = columns.transpose(3, 2, 0, 1, 4, 5).reshape(2, -1, cols)
    normed_cols, cotan_cols = columns[0], columns[1]

    float_units, half_units = ((group, units), jnp.float32), ((group, units), jnp.bfloat16)
    half_width = ((group, width), jnp.bfloat16)
    core_width = ((rows * chips, width), jnp.bfloat16)
    step, count = chunk(width, 384, 128), len(token_pieces)
    hidden, slope, normed_all = call(
        functools.partial(preact_kernel, step, count),
        (*token_pieces, gain_row, up_weight),
        [WHOLE] * (count + 1) + [STAYS],
        (half_units, float_units, half_width),
        up_weight,
        step,
        (pltpu.VMEM(*float_units),),
    )
    span_of, count = chunk(units, 512, 128), len(cotan_pieces)
    step = chunk(span_of, 256, 128)
    (pre_grad,) = call(
        functools.partial(hidgrad_kernel, step, span_of, count),
        (*cotan_pieces, down_weight, slope),
        [WHOLE] * count + [STAYS, WHOLE],
        (half_units,),
        down_weight,
        step,
        (pltpu.VMEM(*half_width),),
    )
    step = chunk(width, 768, 128)
    mine, other, gain_grad = call(
        functools.partial(normgrad_kernel, step),
        (pre_grad, up_weight, normed_all, gain_row),
        [WHOLE, STAYS, WHOLE, WHOLE],
        (core_width, core_width, ((1, width), jnp.float32)),
        up_weight,
        step,
    )

    hidden_all = jnp.concatenate(replicas(hidden, True), axis=0)
    pre_all = jnp.concatenate(replicas(pre_grad, False), axis=0)

    received = [along_ring(gain_grad, s) for s in range(1, chips)]
    for part in received:
        gain_grad = gain_grad + part
    gain_grad = gain_grad + across(gain_grad)
    for bit in range((n_dp - 1).bit_length()):
        gain_grad = gain_grad + replica(gain_grad, 1 << bit)
    gain_grad = gain_grad.reshape(width) * factor

    total = mine.astype(jnp.float32) + across(other).astype(jnp.float32)
    parts = total.astype(jnp.bfloat16).reshape(chips, rows, width)
    norm_grad = total[:rows]
    for s in range(1, chips):
        norm_grad = norm_grad + along_ring(parts[s], -s).astype(jnp.float32)
    scaled = norm_gain * norm_grad
    input_grad = (
        scaled
        - jnp.mean(scaled, axis=1, keepdims=True)
        - x_hat * jnp.mean(scaled * x_hat, axis=1, keepdims=True)
    ) * inv_std

    down_grad = (contract(hidden_all, cotan_cols, ((0,), (0,))) * factor).astype(jnp.bfloat16)
    up_grad = (contract(normed_cols, pre_all, ((0,), (0,))) * factor).astype(jnp.bfloat16)
    return (input_grad.astype(jnp.bfloat16), up_grad, down_grad, gain_grad)


def solution(mesh):
    placed = (P(("dp", "mp"), None), P(), P(None, "mp"), P("mp", None), P(("dp", "mp"), None))
    return jax.shard_map(
        layer,
        mesh=mesh,
        in_specs=placed,
        out_specs=(P(("dp", "mp"), None), P("dp", "mp"), P("mp", "dp"), P()),
        check_vma=False,
    )
```

```python
import functools
import math

import jax
import jax.numpy as jnp
from jax import lax
from jax.experimental import pallas as pl
from jax.experimental.pallas import tpu as pltpu
from jax.sharding import PartitionSpec as P


def gelu_value(preact):
    return 0.5 * preact * (1.0 + lax.erf(preact * 0.7071067811865476))


def gelu_slope(preact):
    return (
        0.5 * (1.0 + lax.erf(preact * 0.7071067811865476))
        + preact * jnp.exp(-0.5 * preact * preact) * 0.3989422804014327
    )


def swap_perm(size, mask):
    return [(i, i ^ mask) for i in range(size)]


def ring_perm(size, shift):
    chips = size // 2
    order = list(range(0, chips, 2)) + list(range(1, chips, 2))[::-1]
    moved = {order[k]: order[(k + shift) % chips] for k in range(chips)}
    return [(2 * c + core, 2 * moved[c] + core) for c in range(chips) for core in range(2)]


def contract(a, b, dims):
    return lax.dot_general(a, b, (dims, ((), ())), preferred_element_type=jnp.float32)


def normalise(values, gain):
    values = values.astype(jnp.float32)
    centered = values - jnp.mean(values, axis=1, keepdims=True)
    inv_std = lax.rsqrt(jnp.mean(centered * centered, axis=1, keepdims=True) + 1e-06)
    x_hat = centered * inv_std
    return (x_hat * gain).astype(jnp.bfloat16), x_hat, inv_std


def chunk(total, most, unit):
    for parts in range(1, total // unit + 1):
        if total % parts == 0 and total // parts <= most and (total // parts) % unit == 0:
            return total // parts
    return total


WHOLE = pl.BlockSpec(memory_space=pltpu.VMEM)
STAYS = pl.BlockSpec(memory_space=pltpu.HBM)


def call(kernel, operands, outs, grant, flops, extra=(), stay=0):
    moved = sum(o.size * o.dtype.itemsize for o in operands)
    return pl.pallas_call(
        kernel,
        in_specs=[WHOLE] * (len(operands) - stay) + [STAYS] * stay,
        out_specs=[WHOLE] * len(outs),
        out_shape=[jax.ShapeDtypeStruct(*o) if isinstance(o, tuple) else o for o in outs],
        scratch_shapes=extra,
        compiler_params=pltpu.CompilerParams(vmem_limit_bytes=grant * 2**20),
        cost_estimate=pl.CostEstimate(flops=flops, bytes_accessed=moved, transcendentals=0),
    )(*operands)


def fetch_copies(start, weight, held, sems):
    count = sems.shape[0]
    step = held.shape[0] // count
    return [
        pltpu.make_async_copy(
            weight.at[pl.ds(start + part * step, step)], held.at[pl.ds(part * step, step)], sems.at[part]
        )
        for part in range(count)
    ]


def fetch_kernel(start, weight, held, sems):
    copies = fetch_copies(start, weight, held, sems)
    for copy in copies:
        copy.start()
    for copy in copies:
        copy.wait()


def norm_kernel(parts, tokens, cotan, gain, weight, x_hat, scale, blocks, held, sems):
    copies = fetch_copies(0, weight, held, sems)
    for copy in copies:
        copy.start()
    normed, x_hat[...], inv_std = normalise(tokens[...], gain[...])
    scale[...] = jnp.broadcast_to(inv_std, scale.shape)
    cols = normed.shape[1] // parts
    for part in range(parts):
        span = slice(part * cols, (part + 1) * cols)
        blocks[part, 0] = normed[:, span]
        blocks[part, 1] = cotan[:, span]
    for copy in copies:
        copy.wait()


def preact_kernel(step, count, *refs):
    pieces, rest = refs[:count], refs[count:]
    gain, first, second, down, hidden, slope, normed, held, sems = rest
    copies = fetch_copies(0, down, held, sems)
    for copy in copies:
        copy.start()
    cut = first.shape[0]
    row = 0
    for piece in pieces:
        normed[row : row + piece.shape[0], :] = normalise(piece[...], gain[...])[0]
        row += piece.shape[0]

    def body(part, carry):
        span = pl.ds(pl.multiple_of(part * step, step), step)
        total = contract(normed[:, :cut], first[:, span], ((1,), (0,)))
        total += contract(normed[:, cut:], second[:, span], ((1,), (0,)))
        hidden[:, span] = gelu_value(total).astype(jnp.bfloat16)
        slope[:, span] = gelu_slope(total)
        return carry

    lax.fori_loop(0, first.shape[1] // step, body, 0)
    for copy in copies:
        copy.wait()


def hidgrad_kernel(step, count, *refs):
    pieces, (first, slope, weight, pre, cotan, held, sems) = refs[:count], refs[count:]
    slots = held.shape[0]
    parts = weight.shape[0] // step

    def copy(part):
        start = part * step if isinstance(part, int) else pl.multiple_of(part * step, step)
        slot = lax.rem(part, slots)
        return pltpu.make_async_copy(weight.at[pl.ds(start, step)], held.at[slot], sems.at[part])

    def product(part_of_weight, part):
        span = pl.ds(pl.multiple_of(part * step, step), step)
        hid_grad = contract(part_of_weight[...], cotan[...], ((1,), (1,))).T
        pre[:, span] = (hid_grad * slope[:, span]).astype(jnp.bfloat16)

    if parts > 1:
        copy(1).start()
    row = 0
    for piece in pieces:
        cotan[row : row + piece.shape[0], :] = piece[...]
        row += piece.shape[0]
    product(first, 0)

    def body(part, carry):
        copy(part).wait()

        @pl.when(part + 1 < parts)
        def _():
            copy(part + 1).start()

        product(held.at[lax.rem(part, slots)], part)
        return carry

    lax.fori_loop(1, parts, body, 0)


def normgrad_kernel(step, pre, first, second, normed, gain, mine, other, gain_part):
    half = mine.shape[0]

    def half_of(weight, offset):
        def body(part, carry):
            rows = pl.ds(pl.multiple_of(part * step, step), step)
            span = pl.ds(pl.multiple_of(offset + part * step, 128), step)
            grad = contract(weight[rows, :], pre[...], ((1,), (1,))).T
            mine[:, span] = grad[:half].astype(jnp.bfloat16)
            other[:, span] = grad[half:].astype(jnp.bfloat16)
            x_hat = normed[:, span].astype(jnp.float32) / gain[:, span]
            gain_part[:, span] = jnp.sum(grad * x_hat, axis=0, keepdims=True)
            return carry

        lax.fori_loop(0, weight.shape[0] // step, body, 0)

    half_of(first, 0)
    half_of(second, first.shape[0])


def layer(tokens, norm_gain, up_weight, down_weight, out_grad):
    up_weight = pltpu.with_memory_space_constraint(up_weight, pltpu.HBM)
    down_weight = pltpu.with_memory_space_constraint(down_weight, pltpu.HBM)
    n_dp, n_mp = lax.axis_size("dp"), lax.axis_size("mp")
    chips = n_mp // 2
    rows, width = tokens.shape
    units = up_weight.shape[1]
    group = rows * n_mp
    cols = width // n_dp
    me = lax.axis_index("dp")
    factor = 1.0 / math.sqrt(group * n_dp)

    def along_ring(array, shift=1):
        return lax.ppermute(array, "mp", ring_perm(n_mp, shift))

    def across(array):
        return lax.ppermute(array, "mp", swap_perm(n_mp, 1))

    def replica(array, mask):
        return lax.ppermute(array, "dp", swap_perm(n_dp, mask))

    def spread(own, relayed):
        pieces = [own]
        for s in range(1, chips):
            if relayed:
                pieces.append(along_ring(pieces[-1]))
            else:
                pieces.append(along_ring(own, s))
        return pieces, [across(p) for p in pieces]

    def gathered(own, relayed):
        mine, other = spread(own, relayed)
        return mine + other if rows % 16 == 0 else [jnp.concatenate(mine + other, axis=0)]

    def replicas(own, low):
        out = [own]
        for k in range(1, n_dp):
            bit = (k & -k) if low else 1 << (k.bit_length() - 1)
            out.append(replica(out[k ^ bit], bit))
        return out

    token_pieces = gathered(tokens, True)
    cotan_pieces = gathered(out_grad, False)
    gain_row = norm_gain.reshape(1, width)
    first = width // 2
    fetch_sems = [pltpu.SemaphoreType.DMA((4,))]
    x_hat, scale, blocks, up_first = pl.pallas_call(
        functools.partial(norm_kernel, n_dp),
        in_specs=[WHOLE] * 3 + [STAYS],
        out_specs=[WHOLE] * 4,
        scratch_shapes=fetch_sems,
        compiler_params=pltpu.CompilerParams(vmem_limit_bytes=5 * 2**20),
        out_shape=[
            jax.ShapeDtypeStruct((rows, width), jnp.float32),
            jax.ShapeDtypeStruct((rows, 128), jnp.float32),
            jax.ShapeDtypeStruct((n_dp, 2, rows, cols), jnp.bfloat16),
            pltpu.VMEM((first, units), jnp.bfloat16),
        ],
        name="ln",
    )(tokens, out_grad, gain_row, up_weight)
    inv_std = scale[:, :1]
    up_second = pl.pallas_call(
        functools.partial(fetch_kernel, first),
        in_specs=[STAYS],
        out_specs=WHOLE,
        scratch_shapes=fetch_sems,
        compiler_params=pltpu.CompilerParams(vmem_limit_bytes=2 * 2**20),
        out_shape=pltpu.VMEM((width - first, units), jnp.bfloat16),
        name="fetch",
    )(up_weight)

    def column_shards(k):
        both = lax.dynamic_index_in_dim(blocks, me ^ k, 0, keepdims=False)
        return replica(both, k) if k else both

    shard_list = [column_shards(k) for k in range(n_dp)]
    shard = jnp.stack(shard_list)
    shards_mine, shards_other = spread(shard, False)
    columns = jnp.stack([jnp.stack(shards_mine), jnp.stack(shards_other)])
    columns = columns.transpose(3, 2, 0, 1, 4, 5).reshape(2, -1, cols)
    normed_cols, cotan_cols = columns[0], columns[1]

    float_units, half_units = ((group, units), jnp.float32), ((group, units), jnp.bfloat16)
    half_width = ((group, width), jnp.bfloat16)
    core_width = ((rows * chips, width), jnp.bfloat16)
    flops = 2 * group * width * units
    part_rows = chunk(units, 512, 128)
    hidden, slope, normed_all, down_first = call(
        functools.partial(preact_kernel, chunk(units, 512, 128), len(token_pieces)),
        (*token_pieces, gain_row, up_first, up_second, down_weight),
        (half_units, float_units, half_width, pltpu.VMEM((part_rows, width), jnp.bfloat16)),
        5,
        flops,
        fetch_sems,
        1,
    )
    step = part_rows
    (pre_grad,) = call(
        functools.partial(hidgrad_kernel, step, len(cotan_pieces)),
        (*cotan_pieces, down_first, slope, down_weight),
        (half_units,),
        16,
        flops,
        (
            pltpu.VMEM(*half_width),
            pltpu.VMEM((2, step, width), jnp.bfloat16),
            pltpu.SemaphoreType.DMA((units // step,)),
        ),
        1,
    )
    mine, other, gain_grad = call(
        functools.partial(normgrad_kernel, chunk(first, 1536, 128)),
        (pre_grad, up_first, up_second, normed_all, gain_row),
        (core_width, core_width, ((1, width), jnp.float32)),
        5,
        flops,
    )

    hidden_all = jnp.concatenate(replicas(hidden, True), axis=0)
    pre_all = jnp.concatenate(replicas(pre_grad, False), axis=0)

    received = [along_ring(gain_grad, s) for s in range(1, chips)]
    for part in received:
        gain_grad = gain_grad + part
    gain_grad = gain_grad + across(gain_grad)
    for bit in range((n_dp - 1).bit_length()):
        gain_grad = gain_grad + replica(gain_grad, 1 << bit)
    gain_grad = gain_grad.reshape(width) * factor

    total = mine.astype(jnp.float32) + across(other).astype(jnp.float32)
    parts = total.astype(jnp.bfloat16).reshape(chips, rows, width)
    norm_grad = total[:rows]
    for s in range(1, chips):
        norm_grad = norm_grad + along_ring(parts[s], -s).astype(jnp.float32)
    scaled = norm_gain * norm_grad
    input_grad = (
        scaled
        - jnp.mean(scaled, axis=1, keepdims=True)
        - x_hat * jnp.mean(scaled * x_hat, axis=1, keepdims=True)
    ) * inv_std

    down_grad = (contract(hidden_all, cotan_cols, ((0,), (0,))) * factor).astype(jnp.bfloat16)
    up_grad = (contract(normed_cols, pre_all, ((0,), (0,))) * factor).astype(jnp.bfloat16)
    return (input_grad.astype(jnp.bfloat16), up_grad, down_grad, gain_grad)


def solution(mesh):
    placed = (P(("dp", "mp"), None), P(), P(None, "mp"), P("mp", None), P(("dp", "mp"), None))
    return jax.shard_map(
        layer,
        mesh=mesh,
        in_specs=placed,
        out_specs=(P(("dp", "mp"), None), P("dp", "mp"), P("mp", "dp"), P()),
        check_vma=False,
    )
```

```python
import functools
import math

import jax
import jax.numpy as jnp
from jax import lax
from jax.experimental import pallas as pl
from jax.experimental.pallas import tpu as pltpu
from jax.sharding import PartitionSpec as P


def gelu_value(preact):
    return 0.5 * preact * (1.0 + lax.erf(preact * 0.7071067811865476))


def gelu_slope(preact):
    return (
        0.5 * (1.0 + lax.erf(preact * 0.7071067811865476))
        + preact * jnp.exp(-0.5 * preact * preact) * 0.3989422804014327
    )


def swap_perm(size, mask):
    return [(i, i ^ mask) for i in range(size)]


def ring_perm(size, shift):
    chips = size // 2
    order = list(range(0, chips, 2)) + list(range(1, chips, 2))[::-1]
    moved = {order[k]: order[(k + shift) % chips] for k in range(chips)}
    return [(2 * c + core, 2 * moved[c] + core) for c in range(chips) for core in range(2)]


def contract(a, b, dims):
    return lax.dot_general(a, b, (dims, ((), ())), preferred_element_type=jnp.float32)


def normalise(values, gain):
    values = values.astype(jnp.float32)
    centered = values - jnp.mean(values, axis=1, keepdims=True)
    inv_std = lax.rsqrt(jnp.mean(centered * centered, axis=1, keepdims=True) + 1e-06)
    x_hat = centered * inv_std
    return (x_hat * gain).astype(jnp.bfloat16), x_hat, inv_std


def chunk(total, most, unit):
    for parts in range(1, total // unit + 1):
        if total % parts == 0 and total // parts <= most and (total // parts) % unit == 0:
            return total // parts
    return total


WHOLE = pl.BlockSpec(memory_space=pltpu.VMEM)
STAYS = pl.BlockSpec(memory_space=pltpu.HBM)


def call(kernel, operands, outs, grant, flops, extra=(), stay=0):
    moved = sum(o.size * o.dtype.itemsize for o in operands)
    return pl.pallas_call(
        kernel,
        in_specs=[WHOLE] * (len(operands) - stay) + [STAYS] * stay,
        out_specs=[WHOLE] * len(outs),
        out_shape=[jax.ShapeDtypeStruct(*o) if isinstance(o, tuple) else o for o in outs],
        scratch_shapes=extra,
        compiler_params=pltpu.CompilerParams(vmem_limit_bytes=grant * 2**20),
        cost_estimate=pl.CostEstimate(flops=flops, bytes_accessed=moved, transcendentals=0),
    )(*operands)


def fetch_copies(start, weight, held, sems):
    count = sems.shape[0]
    step = held.shape[0] // count
    return [
        pltpu.make_async_copy(
            weight.at[pl.ds(start + part * step, step)], held.at[pl.ds(part * step, step)], sems.at[part]
        )
        for part in range(count)
    ]


def fetch_kernel(start, weight, held, sems):
    copies = fetch_copies(start, weight, held, sems)
    for copy in copies:
        copy.start()
    for copy in copies:
        copy.wait()


def norm_kernel(tokens, gain, weight, x_hat, scale, held, sems):
    copies = fetch_copies(0, weight, held, sems)
    for copy in copies:
        copy.start()
    _, x_hat[...], inv_std = normalise(tokens[...], gain[...])
    scale[...] = jnp.broadcast_to(inv_std, scale.shape)
    for copy in copies:
        copy.wait()


def preact_kernel(step, count, *refs):
    pieces, rest = refs[:count], refs[count:]
    gain, first, second, down, hidden, slope, normed, held, sems = rest
    copies = fetch_copies(0, down, held, sems)
    for copy in copies:
        copy.start()
    cut = first.shape[0]
    row = 0
    for piece in pieces:
        normed[row : row + piece.shape[0], :] = normalise(piece[...], gain[...])[0]
        row += piece.shape[0]

    def body(part, carry):
        span = pl.ds(pl.multiple_of(part * step, step), step)
        total = contract(normed[:, :cut], first[:, span], ((1,), (0,)))
        total += contract(normed[:, cut:], second[:, span], ((1,), (0,)))
        hidden[:, span] = gelu_value(total).astype(jnp.bfloat16)
        slope[:, span] = gelu_slope(total)
        return carry

    lax.fori_loop(0, first.shape[1] // step, body, 0)
    for copy in copies:
        copy.wait()


def hidgrad_kernel(step, count, *refs):
    pieces, (first, slope, weight, pre, cotan, held, sems) = refs[:count], refs[count:]
    slots = held.shape[0]
    parts = weight.shape[0] // step

    def copy(part):
        start = part * step if isinstance(part, int) else pl.multiple_of(part * step, step)
        slot = lax.rem(part, slots)
        return pltpu.make_async_copy(weight.at[pl.ds(start, step)], held.at[slot], sems.at[part])

    def product(part_of_weight, part):
        span = pl.ds(pl.multiple_of(part * step, step), step)
        hid_grad = contract(part_of_weight[...], cotan[...], ((1,), (1,))).T
        pre[:, span] = (hid_grad * slope[:, span]).astype(jnp.bfloat16)

    if parts > 1:
        copy(1).start()
    row = 0
    for piece in pieces:
        cotan[row : row + piece.shape[0], :] = piece[...]
        row += piece.shape[0]
    product(first, 0)

    def body(part, carry):
        copy(part).wait()

        @pl.when(part + 1 < parts)
        def _():
            copy(part + 1).start()

        product(held.at[lax.rem(part, slots)], part)
        return carry

    lax.fori_loop(1, parts, body, 0)


def normgrad_kernel(step, pre, first, second, normed, gain, mine, other, gain_part):
    half = mine.shape[0]

    def half_of(weight, offset):
        def body(part, carry):
            rows = pl.ds(pl.multiple_of(part * step, step), step)
            span = pl.ds(pl.multiple_of(offset + part * step, 128), step)
            grad = contract(weight[rows, :], pre[...], ((1,), (1,))).T
            mine[:, span] = grad[:half].astype(jnp.bfloat16)
            other[:, span] = grad[half:].astype(jnp.bfloat16)
            x_hat = normed[:, span].astype(jnp.float32) / gain[:, span]
            gain_part[:, span] = jnp.sum(grad * x_hat, axis=0, keepdims=True)
            return carry

        lax.fori_loop(0, weight.shape[0] // step, body, 0)

    half_of(first, 0)
    half_of(second, first.shape[0])


def layer(tokens, norm_gain, up_weight, down_weight, out_grad):
    up_weight = pltpu.with_memory_space_constraint(up_weight, pltpu.HBM)
    down_weight = pltpu.with_memory_space_constraint(down_weight, pltpu.HBM)
    n_dp, n_mp = lax.axis_size("dp"), lax.axis_size("mp")
    chips = n_mp // 2
    rows, width = tokens.shape
    units = up_weight.shape[1]
    group = rows * n_mp
    cols = width // n_dp
    me = lax.axis_index("dp")
    factor = 1.0 / math.sqrt(group * n_dp)

    def along_ring(array, shift=1):
        return lax.ppermute(array, "mp", ring_perm(n_mp, shift))

    def across(array):
        return lax.ppermute(array, "mp", swap_perm(n_mp, 1))

    def replica(array, mask):
        return lax.ppermute(array, "dp", swap_perm(n_dp, mask))

    def spread(own, relayed):
        pieces = [own]
        for s in range(1, chips):
            if relayed:
                pieces.append(along_ring(pieces[-1]))
            else:
                pieces.append(along_ring(own, s))
        return pieces, [across(p) for p in pieces]

    def gathered(own, relayed):
        mine, other = spread(own, relayed)
        return mine + other if rows % 16 == 0 else [jnp.concatenate(mine + other, axis=0)]

    def replicas(own, low):
        out = [own]
        for k in range(1, n_dp):
            bit = (k & -k) if low else 1 << (k.bit_length() - 1)
            out.append(replica(out[k ^ bit], bit))
        return out

    token_pieces = gathered(tokens, True)
    cotan_pieces = gathered(out_grad, False)
    gain_row = norm_gain.reshape(1, width)
    first = width // 2
    fetch_sems = [pltpu.SemaphoreType.DMA((4,))]
    x_hat, scale, up_first = pl.pallas_call(
        norm_kernel,
        in_specs=[WHOLE] * 2 + [STAYS],
        out_specs=[WHOLE] * 3,
        scratch_shapes=fetch_sems,
        compiler_params=pltpu.CompilerParams(vmem_limit_bytes=5 * 2**20),
        out_shape=[
            jax.ShapeDtypeStruct((rows, width), jnp.float32),
            jax.ShapeDtypeStruct((rows, 128), jnp.float32),
            pltpu.VMEM((first, units), jnp.bfloat16),
        ],
        name="ln",
    )(tokens, gain_row, up_weight)
    inv_std = scale[:, :1]
    up_second = pl.pallas_call(
        functools.partial(fetch_kernel, first),
        in_specs=[STAYS],
        out_specs=WHOLE,
        scratch_shapes=fetch_sems,
        compiler_params=pltpu.CompilerParams(vmem_limit_bytes=2 * 2**20),
        out_shape=pltpu.VMEM((width - first, units), jnp.bfloat16),
        name="fetch",
    )(up_weight)

    def block_of(array, k):
        return lax.dynamic_slice_in_dim(array, (me ^ k) * cols, cols, axis=1)

    def column_shards(k):
        block = block_of(out_grad, k)
        return replica(block, k) if k else block

    shard_list = [column_shards(k) for k in range(n_dp)]
    shard = jnp.stack(shard_list)
    shards_mine, shards_other = spread(shard, False)
    columns = jnp.stack([jnp.stack(shards_mine), jnp.stack(shards_other)])
    cotan_cols = columns.transpose(2, 0, 1, 3, 4).reshape(-1, cols)

    float_units, half_units = ((group, units), jnp.float32), ((group, units), jnp.bfloat16)
    half_width = ((group, width), jnp.bfloat16)
    core_width = ((rows * chips, width), jnp.bfloat16)
    flops = 2 * group * width * units
    part_rows = chunk(units, 512, 128)
    hidden, slope, normed_all, down_first = call(
        functools.partial(preact_kernel, chunk(units, 512, 128), len(token_pieces)),
        (*token_pieces, gain_row, up_first, up_second, down_weight),
        (half_units, float_units, half_width, pltpu.VMEM((part_rows, width), jnp.bfloat16)),
        5,
        flops,
        fetch_sems,
        1,
    )
    step = part_rows
    (pre_grad,) = call(
        functools.partial(hidgrad_kernel, step, len(cotan_pieces)),
        (*cotan_pieces, down_first, slope, down_weight),
        (half_units,),
        16,
        flops,
        (
            pltpu.VMEM(*half_width),
            pltpu.VMEM((2, step, width), jnp.bfloat16),
            pltpu.SemaphoreType.DMA((units // step,)),
        ),
        1,
    )
    mine, other, gain_grad = call(
        functools.partial(normgrad_kernel, chunk(first, 1536, 128)),
        (pre_grad, up_first, up_second, normed_all, gain_row),
        (core_width, core_width, ((1, width), jnp.float32)),
        5,
        flops,
    )

    hidden_all = jnp.concatenate(replicas(hidden, True), axis=0)
    pre_all = jnp.concatenate(replicas(pre_grad, False), axis=0)

    half = rows * chips
    normed_parts = [block_of(normed_all, 0)]
    for k in range(1, n_dp):
        block = replica(block_of(normed_all[:half], k), k)
        normed_parts += [block, across(block)]
    normed_cols = jnp.concatenate(normed_parts, axis=0)

    received = [along_ring(gain_grad, s) for s in range(1, chips)]
    for part in received:
        gain_grad = gain_grad + part
    for bit in range((n_dp - 1).bit_length()):
        gain_grad = gain_grad + replica(gain_grad, 1 << bit)
    gain_grad = gain_grad + across(gain_grad)
    gain_grad = gain_grad.reshape(width) * factor

    total = mine.astype(jnp.float32) + across(other).astype(jnp.float32)
    parts = total.astype(jnp.bfloat16).reshape(chips, rows, width)
    norm_grad = total[:rows]
    for s in range(1, chips):
        norm_grad = norm_grad + along_ring(parts[s], -s).astype(jnp.float32)
    scaled = norm_gain * norm_grad
    input_grad = (
        scaled
        - jnp.mean(scaled, axis=1, keepdims=True)
        - x_hat * jnp.mean(scaled * x_hat, axis=1, keepdims=True)
    ) * inv_std

    down_grad = (contract(hidden_all, cotan_cols, ((0,), (0,))) * factor).astype(jnp.bfloat16)
    up_grad = (contract(normed_cols, pre_all, ((0,), (0,))) * factor).astype(jnp.bfloat16)
    return (input_grad.astype(jnp.bfloat16), up_grad, down_grad, gain_grad)


def solution(mesh):
    placed = (P(("dp", "mp"), None), P(), P(None, "mp"), P("mp", None), P(("dp", "mp"), None))
    return jax.shard_map(
        layer,
        mesh=mesh,
        in_specs=placed,
        out_specs=(P(("dp", "mp"), None), P("dp", "mp"), P("mp", "dp"), P()),
        check_vma=False,
    )
```

```python
import functools
import math

import jax
import jax.numpy as jnp
from jax import lax
from jax.experimental import pallas as pl
from jax.experimental.pallas import tpu as pltpu
from jax.sharding import PartitionSpec as P


def gelu_value(preact):
    return 0.5 * preact * (1.0 + lax.erf(preact * 0.7071067811865476))


def gelu_slope(preact):
    return (
        0.5 * (1.0 + lax.erf(preact * 0.7071067811865476))
        + preact * jnp.exp(-0.5 * preact * preact) * 0.3989422804014327
    )


def swap_perm(size, mask):
    return [(i, i ^ mask) for i in range(size)]


def ring_perm(size, shift):
    chips = size // 2
    order = list(range(0, chips, 2)) + list(range(1, chips, 2))[::-1]
    moved = {order[k]: order[(k + shift) % chips] for k in range(chips)}
    return [(2 * c + core, 2 * moved[c] + core) for c in range(chips) for core in range(2)]


def contract(a, b, dims):
    return lax.dot_general(a, b, (dims, ((), ())), preferred_element_type=jnp.float32)


def normalise(values, gain):
    values = values.astype(jnp.float32)
    centered = values - jnp.mean(values, axis=1, keepdims=True)
    inv_std = lax.rsqrt(jnp.mean(centered * centered, axis=1, keepdims=True) + 1e-06)
    x_hat = centered * inv_std
    return (x_hat * gain).astype(jnp.bfloat16), x_hat, inv_std


def chunk(total, most, unit):
    for parts in range(1, total // unit + 1):
        if total % parts == 0 and total // parts <= most and (total // parts) % unit == 0:
            return total // parts
    return total


WHOLE = pl.BlockSpec(memory_space=pltpu.VMEM)
STAYS = pl.BlockSpec(memory_space=pltpu.HBM)


def call(kernel, operands, outs, grant, flops, extra=(), stay=0):
    moved = sum(o.size * o.dtype.itemsize for o in operands)
    return pl.pallas_call(
        kernel,
        in_specs=[WHOLE] * (len(operands) - stay) + [STAYS] * stay,
        out_specs=[WHOLE] * len(outs),
        out_shape=[jax.ShapeDtypeStruct(*o) if isinstance(o, tuple) else o for o in outs],
        scratch_shapes=extra,
        compiler_params=pltpu.CompilerParams(vmem_limit_bytes=grant * 2**20),
        cost_estimate=pl.CostEstimate(flops=flops, bytes_accessed=moved, transcendentals=0),
    )(*operands)


def fetch_copies(start, weight, held, sems):
    count = sems.shape[0]
    step = held.shape[0] // count
    return [
        pltpu.make_async_copy(
            weight.at[pl.ds(start + part * step, step)], held.at[pl.ds(part * step, step)], sems.at[part]
        )
        for part in range(count)
    ]


def fetch_kernel(start, weight, held, sems):
    copies = fetch_copies(start, weight, held, sems)
    for copy in copies:
        copy.start()
    for copy in copies:
        copy.wait()


def norm_kernel(tokens, gain, weight, x_hat, scale, held, sems, rows, row, row_sems):
    copies = fetch_copies(0, weight, held, sems)
    small = [
        pltpu.make_async_copy(tokens, rows, row_sems.at[0]),
        pltpu.make_async_copy(gain, row, row_sems.at[1]),
    ]
    for copy in small + copies:
        copy.start()
    for copy in small:
        copy.wait()
    _, x_hat[...], inv_std = normalise(rows[...], row[...])
    scale[...] = jnp.broadcast_to(inv_std, scale.shape)
    for copy in copies:
        copy.wait()


def preact_kernel(step, count, *refs):
    pieces, rest = refs[:count], refs[count:]
    gain, first, second, down, hidden, slope, normed, held, sems = rest
    copies = fetch_copies(0, down, held, sems)
    for copy in copies:
        copy.start()
    cut = first.shape[0]
    row = 0
    for piece in pieces:
        normed[row : row + piece.shape[0], :] = normalise(piece[...], gain[...])[0]
        row += piece.shape[0]

    def body(part, carry):
        span = pl.ds(pl.multiple_of(part * step, step), step)
        total = contract(normed[:, :cut], first[:, span], ((1,), (0,)))
        total += contract(normed[:, cut:], second[:, span], ((1,), (0,)))
        hidden[:, span] = gelu_value(total).astype(jnp.bfloat16)
        slope[:, span] = gelu_slope(total)
        return carry

    lax.fori_loop(0, first.shape[1] // step, body, 0)
    for copy in copies:
        copy.wait()


def hidgrad_kernel(step, count, *refs):
    pieces, (first, slope, weight, pre, cotan, held, sems) = refs[:count], refs[count:]
    slots = held.shape[0]
    parts = weight.shape[0] // step

    def copy(part):
        start = part * step if isinstance(part, int) else pl.multiple_of(part * step, step)
        slot = lax.rem(part, slots)
        return pltpu.make_async_copy(weight.at[pl.ds(start, step)], held.at[slot], sems.at[part])

    def product(part_of_weight, part):
        span = pl.ds(pl.multiple_of(part * step, step), step)
        hid_grad = contract(part_of_weight[...], cotan[...], ((1,), (1,))).T
        pre[:, span] = (hid_grad * slope[:, span]).astype(jnp.bfloat16)

    if parts > 1:
        copy(1).start()
    row = 0
    for piece in pieces:
        cotan[row : row + piece.shape[0], :] = piece[...]
        row += piece.shape[0]
    product(first, 0)

    def body(part, carry):
        copy(part).wait()

        @pl.when(part + 1 < parts)
        def _():
            copy(part + 1).start()

        product(held.at[lax.rem(part, slots)], part)
        return carry

    lax.fori_loop(1, parts, body, 0)


def normgrad_kernel(step, pre, first, second, normed, gain, mine, other, gain_part):
    half = mine.shape[0]

    def half_of(weight, offset):
        def body(part, carry):
            rows = pl.ds(pl.multiple_of(part * step, step), step)
            span = pl.ds(pl.multiple_of(offset + part * step, 128), step)
            grad = contract(weight[rows, :], pre[...], ((1,), (1,))).T
            mine[:, span] = grad[:half].astype(jnp.bfloat16)
            other[:, span] = grad[half:].astype(jnp.bfloat16)
            x_hat = normed[:, span].astype(jnp.float32) / gain[:, span]
            gain_part[:, span] = jnp.sum(grad * x_hat, axis=0, keepdims=True)
            return carry

        lax.fori_loop(0, weight.shape[0] // step, body, 0)

    half_of(first, 0)
    half_of(second, first.shape[0])


def layer(tokens, norm_gain, up_weight, down_weight, out_grad):
    up_weight = pltpu.with_memory_space_constraint(up_weight, pltpu.HBM)
    down_weight = pltpu.with_memory_space_constraint(down_weight, pltpu.HBM)
    n_dp, n_mp = lax.axis_size("dp"), lax.axis_size("mp")
    chips = n_mp // 2
    rows, width = tokens.shape
    units = up_weight.shape[1]
    group = rows * n_mp
    cols = width // n_dp
    me = lax.axis_index("dp")
    factor = 1.0 / math.sqrt(group * n_dp)

    def along_ring(array, shift=1):
        return lax.ppermute(array, "mp", ring_perm(n_mp, shift))

    def across(array):
        return lax.ppermute(array, "mp", swap_perm(n_mp, 1))

    def replica(array, mask):
        return lax.ppermute(array, "dp", swap_perm(n_dp, mask))

    def spread(own, relayed):
        pieces = [own]
        for s in range(1, chips):
            if relayed:
                pieces.append(along_ring(pieces[-1]))
            else:
                pieces.append(along_ring(own, s))
        return pieces, [across(p) for p in pieces]

    def gathered(own, relayed):
        mine, other = spread(own, relayed)
        return mine + other if rows % 16 == 0 else [jnp.concatenate(mine + other, axis=0)]

    def replicas(own, low):
        out = [own]
        for k in range(1, n_dp):
            bit = (k & -k) if low else 1 << (k.bit_length() - 1)
            out.append(replica(out[k ^ bit], bit))
        return out

    token_pieces = gathered(tokens, True)
    cotan_pieces = gathered(out_grad, False)
    gain_row = norm_gain.reshape(1, width)
    first = width // 2
    fetch_sems = [pltpu.SemaphoreType.DMA((4,))]
    x_hat, scale, up_first = pl.pallas_call(
        norm_kernel,
        in_specs=[STAYS] * 3,
        out_specs=[WHOLE] * 3,
        scratch_shapes=[
            *fetch_sems,
            pltpu.VMEM(tokens.shape, jnp.bfloat16),
            pltpu.VMEM(gain_row.shape, jnp.float32),
            pltpu.SemaphoreType.DMA((2,)),
        ],
        compiler_params=pltpu.CompilerParams(vmem_limit_bytes=5 * 2**20),
        out_shape=[
            jax.ShapeDtypeStruct((rows, width), jnp.float32),
            jax.ShapeDtypeStruct((rows, 128), jnp.float32),
            pltpu.VMEM((first, units), jnp.bfloat16),
        ],
        name="ln",
    )(*(pltpu.with_memory_space_constraint(a, pltpu.HBM) for a in (tokens, gain_row)), up_weight)
    inv_std = scale[:, :1]
    up_second = pl.pallas_call(
        functools.partial(fetch_kernel, first),
        in_specs=[STAYS],
        out_specs=WHOLE,
        scratch_shapes=fetch_sems,
        compiler_params=pltpu.CompilerParams(vmem_limit_bytes=2 * 2**20),
        out_shape=pltpu.VMEM((width - first, units), jnp.bfloat16),
        name="fetch",
    )(up_weight)

    def block_of(array, k):
        return lax.dynamic_slice_in_dim(array, (me ^ k) * cols, cols, axis=1)

    def column_shards(k):
        block = block_of(out_grad, k)
        return replica(block, k) if k else block

    shard_list = [column_shards(k) for k in range(n_dp)]
    shard = jnp.stack(shard_list)
    shards_mine, shards_other = spread(shard, False)
    columns = jnp.stack([jnp.stack(shards_mine), jnp.stack(shards_other)])
    cotan_cols = columns.transpose(2, 0, 1, 3, 4).reshape(-1, cols)

    float_units, half_units = ((group, units), jnp.float32), ((group, units), jnp.bfloat16)
    half_width = ((group, width), jnp.bfloat16)
    core_width = ((rows * chips, width), jnp.bfloat16)
    flops = 2 * group * width * units
    part_rows = chunk(units, 512, 128)
    hidden, slope, normed_all, down_first = call(
        functools.partial(preact_kernel, chunk(units, 1024, 128), len(token_pieces)),
        (*token_pieces, gain_row, up_first, up_second, down_weight),
        (half_units, float_units, half_width, pltpu.VMEM((part_rows, width), jnp.bfloat16)),
        5,
        flops,
        fetch_sems,
        1,
    )
    step = part_rows
    (pre_grad,) = call(
        functools.partial(hidgrad_kernel, step, len(cotan_pieces)),
        (*cotan_pieces, down_first, slope, down_weight),
        (half_units,),
        16,
        flops,
        (
            pltpu.VMEM(*half_width),
            pltpu.VMEM((2, step, width), jnp.bfloat16),
            pltpu.SemaphoreType.DMA((units // step,)),
        ),
        1,
    )
    mine, other, gain_grad = call(
        functools.partial(normgrad_kernel, chunk(first, 3072, 128)),
        (pre_grad, up_first, up_second, normed_all, gain_row),
        (core_width, core_width, ((1, width), jnp.float32)),
        5,
        flops,
    )

    hidden_all = jnp.concatenate(replicas(hidden, True), axis=0)
    pre_all = jnp.concatenate(replicas(pre_grad, False), axis=0)

    half = rows * chips
    normed_parts = [block_of(normed_all, 0)]
    for k in range(1, n_dp):
        block = replica(block_of(normed_all[:half], k), k)
        normed_parts += [block, across(block)]
    normed_cols = jnp.concatenate(normed_parts, axis=0)

    received = [along_ring(gain_grad, s) for s in range(1, chips)]
    for part in received:
        gain_grad = gain_grad + part
    for bit in range((n_dp - 1).bit_length()):
        part = replica(gain_grad, 1 << bit)
        gain_grad = gain_grad + part
    gain_grad = gain_grad + across(gain_grad)
    gain_grad = gain_grad.reshape(width) * factor

    total = mine.astype(jnp.float32) + across(other).astype(jnp.float32)
    parts = total.astype(jnp.bfloat16).reshape(chips, rows, width)
    norm_grad = total[:rows]
    for s in range(1, chips):
        norm_grad = norm_grad + along_ring(parts[s], -s).astype(jnp.float32)
    scaled = norm_gain * norm_grad
    input_grad = (
        scaled
        - jnp.mean(scaled, axis=1, keepdims=True)
        - x_hat * jnp.mean(scaled * x_hat, axis=1, keepdims=True)
    ) * inv_std

    down_grad = (contract(hidden_all, cotan_cols, ((0,), (0,))) * factor).astype(jnp.bfloat16)
    up_grad = (contract(normed_cols, pre_all, ((0,), (0,))) * factor).astype(jnp.bfloat16)
    return (input_grad.astype(jnp.bfloat16), up_grad, down_grad, gain_grad)


def solution(mesh):
    placed = (P(("dp", "mp"), None), P(), P(None, "mp"), P("mp", None), P(("dp", "mp"), None))
    return jax.shard_map(
        layer,
        mesh=mesh,
        in_specs=placed,
        out_specs=(P(("dp", "mp"), None), P("dp", "mp"), P("mp", "dp"), P()),
        check_vma=False,
    )
```
